32 devices in a mesh: dp: 16 (over z, y, core), mp: 2 (over x).
Axes of the slice: x: 2, y: 2, z: 4, core: 2. Of those that a mesh axis runs over, the one named last changes fastest.
Arguments:
- tokens: bfloat16 [32768, 1024], P(('dp', 'mp')), may hold values from -6 to 6
- w_qkv: bfloat16 [1024, 3, 1024], P('dp', None, 'mp'), may hold values from -0.1875 to 0.1875
- w_out: bfloat16 [1024, 1024], P(('mp', 'dp')), may hold values from -0.1875 to 0.1875
- w_in: bfloat16 [1024, 4096], P('dp', 'mp'), may hold values from -0.1875 to 0.1875
- w_back: bfloat16 [4096, 1024], P(('mp', 'dp')), may hold values from -0.28125 to 0.28125
- gain_attn: bfloat16 [1024], P('dp'), may hold values from 0.25 to 1.75
- gain_post: bfloat16 [1024], P('dp'), may hold values from 0.25 to 1.75
- gain_ffn: bfloat16 [1024], P('dp'), may hold values from 0.25 to 1.75
- gain_mid: bfloat16 [4096], P(('mp', 'dp')), may hold values from 0.25 to 1.75
- head_scale: bfloat16 [16], P('mp'), may hold values from 0.25 to 1.75
- cotangent: bfloat16 [32768, 1024], P(('dp', 'mp')), may hold values from -6 to 6
Outputs:
- output: bfloat16 [32768, 1024], P(('dp', 'mp'))
- grad_tokens: bfloat16 [32768, 1024], P(('dp', 'mp'))
- grad_w_qkv: float32 [1024, 3, 1024], P('dp', None, 'mp')
- grad_w_out: float32 [1024, 1024], P(('mp', 'dp'))
- grad_w_in: float32 [1024, 4096], P('dp', 'mp')
- grad_w_back: float32 [4096, 1024], P(('mp', 'dp'))
- grad_gain_attn: float32 [1024], P(('dp', 'mp'))
- grad_gain_post: float32 [1024], P(('dp', 'mp'))
- grad_gain_ffn: float32 [1024], P(('dp', 'mp'))
- grad_gain_mid: float32 [4096], P(('mp', 'dp'))
- grad_head_scale: float32 [16], P('mp')
The draws below stay inside these ranges and needn't reach their ends.
All inputs are finite; a program needn't handle non-finite values.
Results may differ from the reference program's by a relative error of at most 0.02.
Values may be sent and summed in bfloat16 or wider, within the bound.
No kernel may reach another device: no remote copies, remote signals or barrier semaphores. Data moves between devices by JAX's collectives and lax.ppermute only.
A program may use at most 256 MiB of HBM per device.

```python
import jax
import jax.numpy as jnp
from jax import lax

D = 1024
H = 16
HD = 64
FF = 4096
BLOCK = 256
QBLOCK = 512
SEQ = 2048
TOKENS = 32768


def draw_w_back(key, part):
    own_key = jax.random.fold_in(key, 7151)
    entry_key = jax.random.fold_in(own_key, 1)
    common_key = jax.random.fold_in(own_key, 2)
    position = jnp.arange(FF, dtype=jnp.float32) / FF
    entries = jnp.clip(jax.random.normal(entry_key, (FF, D), jnp.float32), -6.0, 6.0)
    rising = 0.5 * jnp.exp(position * 1.386294)
    common = jnp.clip(jax.random.normal(common_key, (D,), jnp.float32), -4.0, 4.0)
    scale = FF ** (-0.5)
    return (entries * scale + rising[:, None] * common[None, :] * scale).astype(jnp.bfloat16)


def steps_of(rng, shape, cuts, low, high):
    loudness = 1.0
    for dim, blocks in cuts:
        steps = jax.random.uniform(jax.random.fold_in(jax.random.fold_in(rng, 6), dim), (blocks,), jnp.float32, low / len(cuts), high / len(cuts))
        loudness = loudness * jnp.repeat(jnp.exp(steps), shape[dim] // blocks).reshape((-1,) + (1,) * (len(shape) - 1 - dim))
    return loudness


def normal_values(stream_key, shape, width, reach, pieces=(), kind=jnp.bfloat16):
    values = jax.random.normal(stream_key, shape, jnp.float32) * width
    if len(pieces) > 0:
        values = steps_of(stream_key, shape, pieces, -0.22, 0.18) * values
    return jnp.clip(values, min=-reach, max=reach).astype(kind)


def setup_inputs(seed: int = 0) -> dict:
    seeds = jax.random.split(jax.random.key(seed), 12)
    return {
        "tokens": normal_values(seeds[0], (TOKENS, D), 1.0, 6.0, ((0, 32),)),
        "w_qkv": normal_values(seeds[1], (D, 3, D), D ** -0.5, 0.1875, ((0, 16), (2, 2))),
        "w_out": normal_values(seeds[2], (D, D), D ** -0.5, 0.1875, ((0, 32),)),
        "w_in": normal_values(seeds[3], (D, FF), D ** -0.5, 0.1875, ((0, 16), (1, 2))),
        "w_back": draw_w_back(jax.random.fold_in(seeds[11], 71), 0),
        "gain_attn": jnp.clip(1.0 + 0.15 * jax.random.normal(seeds[5], (D,), jnp.float32), 0.25, 1.75).astype(jnp.bfloat16),
        "gain_post": jnp.clip(1.0 + 0.15 * jax.random.normal(seeds[6], (D,), jnp.float32), 0.25, 1.75).astype(jnp.bfloat16),
        "gain_ffn": jnp.clip(1.0 + 0.15 * jax.random.normal(seeds[7], (D,), jnp.float32), 0.25, 1.75).astype(jnp.bfloat16),
        "gain_mid": jnp.clip(1.0 + 0.15 * jax.random.normal(seeds[8], (FF,), jnp.float32), 0.25, 1.75).astype(jnp.bfloat16),
        "head_scale": jnp.clip(1.0 + 0.15 * jax.random.normal(seeds[9], (H,), jnp.float32), 0.25, 1.75).astype(jnp.bfloat16),
        "cotangent": normal_values(seeds[10], (TOKENS, D), 1.0, 6.0, ((0, 32),)),
    }


@jax.custom_vjp
def low(v):
    return lax.optimization_barrier(v.astype(jnp.bfloat16)).astype(jnp.float32)

@jax.custom_vjp
def low_back(v):
    return v

def low_keep(v):
    return (low(v), None)

def low_pass(kept, grad):
    return (grad,)

def back_keep(v):
    return (v, None)

def back_low(kept, grad):
    return (low(grad),)
low.defvjp(low_keep, low_pass)
low_back.defvjp(back_keep, back_low)
NORM_EPS = 1e-05
NEG_FILL = -1e+30

def norm_rows(row_values, gain):
    row_mean = lax.optimization_barrier(jnp.mean(row_values, axis=-1, keepdims=True))
    centred = row_values - row_mean
    spread = lax.optimization_barrier(jnp.mean(centred * centred, axis=-1, keepdims=True))
    return centred * lax.rsqrt(spread + NORM_EPS) * gain

def attention(queries, key_rows, value_rows):
    starts = jnp.arange(SEQ // QBLOCK, dtype=jnp.int32) * QBLOCK

    def one_block(offset):
        query_rows = lax.dynamic_slice_in_dim(queries, offset, QBLOCK, 0)
        raw_scores = jnp.einsum('qhd,khd->hqk', query_rows, key_rows, precision=lax.Precision.HIGHEST) * HD ** (-0.5)
        query_pos = offset + jnp.arange(QBLOCK, dtype=jnp.int32)
        key_pos = jnp.arange(SEQ, dtype=jnp.int32)
        allowed = key_pos[None, :] // BLOCK <= query_pos[:, None] // BLOCK
        scores = low_back(jnp.where(allowed[None], raw_scores, NEG_FILL))
        weights = low(jax.nn.softmax(scores, axis=-1))
        return jnp.einsum('hqk,khd->qhd', weights, value_rows, precision=lax.Precision.HIGHEST)
    blocks = lax.map(jax.checkpoint(one_block), starts)
    return blocks.reshape(SEQ, H, HD)

def layer_seq(inputs, params):
    w_qkv, w_out, w_in, w_back, gain_attn, gain_post, gain_ffn, gain_mid, head_scale = params
    entry_attn = low(norm_rows(inputs, gain_attn))
    projected = jnp.dot(entry_attn, w_qkv.reshape(D, 3 * D), precision=lax.Precision.HIGHEST)
    projected = low(low_back(projected)).reshape(SEQ, 3, H, HD)
    attended = low_back(attention(projected[:, 0], projected[:, 1], projected[:, 2]))
    scaled = low((attended * head_scale[None, :, None]).reshape(SEQ, D))
    mixed_sum = low_back(jnp.dot(scaled, w_out, precision=lax.Precision.HIGHEST))
    middle = inputs + norm_rows(mixed_sum, gain_post)
    entry_ffn = low(norm_rows(middle, gain_ffn))
    upper = low_back(jnp.dot(entry_ffn, w_in, precision=lax.Precision.HIGHEST))
    active = jax.nn.gelu(upper, approximate=False)
    fed_down = low(norm_rows(active, gain_mid))
    lowered = low_back(jnp.dot(fed_down, w_back, precision=lax.Precision.HIGHEST))
    return middle + lowered

def reference(tokens, w_qkv, w_out, w_in, w_back, gain_attn, gain_post, gain_ffn, gain_mid, head_scale, cotangent):
    inputs = tokens.astype(jnp.float32)
    params = tuple((weight_item.astype(jnp.float32) for weight_item in (w_qkv, w_out, w_in, w_back, gain_attn, gain_post, gain_ffn, gain_mid, head_scale)))

    def forward(inputs_all, params_all):
        sequences = inputs_all.reshape(TOKENS // SEQ, SEQ, D)
        results = lax.map(lambda one_seq: layer_seq(one_seq, params_all), sequences)
        return results.reshape(TOKENS, D)
    output, pull_back = jax.vjp(forward, inputs, params)
    grad_inputs, grad_params = pull_back(cotangent.astype(jnp.float32))
    return (output.astype(jnp.bfloat16), grad_inputs.astype(jnp.bfloat16), grad_params[0], grad_params[1], grad_params[2], grad_params[3], grad_params[4], grad_params[5], grad_params[6], grad_params[7], grad_params[8])
```

```python
import functools

import jax
import jax.numpy as jnp
from jax import lax
from jax.experimental import pallas as pl
from jax.experimental.pallas import tpu as pltpu
from jax.sharding import Mesh, PartitionSpec as P

HD = 64
BLOCK = 256
LANES = 128
NORM_EPS = 1e-05
F32 = jnp.float32
BF16 = jnp.bfloat16
WEIGHT_AXES = ("p", "h")
PART_AXES = ("c", "l")
ALL_AXES = ("p", "c", "h", "l")


def dot(a, b, dims=((1,), (0,))):
    return lax.dot_general(a, b, (dims, ((), ())), preferred_element_type=F32)


def attn_forward_kernel(chunks, blocks, offs, *refs):
    q_in, k_in, v_in = (refs[t * chunks : (t + 1) * chunks] for t in range(3))
    scale_ref = refs[3 * chunks]
    rest = refs[3 * chunks + 1 :]
    att_out, scaled_out = rest[:chunks], rest[chunks : 2 * chunks]
    lse_ref, qb, kb, vb, ob = rest[2 * chunks :]
    parity = pl.program_id(1)
    rows = q_in[0].shape[0]

    @pl.when(parity == 0)
    def _():
        for t in range(chunks):
            place = pl.ds(pl.multiple_of(offs[t], BLOCK), rows)
            qb[place, :] = q_in[t][...]
            kb[place, :] = k_in[t][...]
            vb[place, :] = v_in[t][...]

    lane_head = lax.broadcasted_iota(jnp.int32, (BLOCK, LANES), 1) // HD
    mine = lane_head == parity
    for i in range(blocks):
        here = slice(i * BLOCK, (i + 1) * BLOCK)
        keys = slice(0, (i + 1) * BLOCK)
        q = jnp.where(mine, qb[here, :] * BF16(HD**-0.5), BF16(0))
        scores = dot(q, kb[keys, :], ((1,), (1,)))
        top = jnp.max(scores, axis=1, keepdims=True)
        weights = jnp.exp(scores - top)
        total = jnp.sum(weights, axis=1, keepdims=True)
        out = dot(weights.astype(BF16), vb[keys, :]) / total
        lse = jnp.broadcast_to(top + jnp.log(total), (BLOCK, LANES))
        lse_ref[0, :, here] = lse.T[:8, :]
        ob[here, :] = jnp.where(mine, out, ob[here, :])

    @pl.when(parity == 1)
    def _():
        for t in range(chunks):
            place = pl.ds(pl.multiple_of(offs[t], BLOCK), rows)
            out = ob[place, :]
            att_out[t][...] = out.astype(BF16)
            scaled_out[t][...] = (out * scale_ref[...]).astype(BF16)


def attn_forward(offs, projected, columns):
    chunks = len(projected)
    rows, width = projected[0].shape[0], projected[0].shape[1] // 3
    total, pairs = rows * chunks, width // LANES

    def column(t):
        return pl.BlockSpec((rows, LANES), lambda j, k, o: (0, t * pairs + j))

    row_specs = [column(t) for t in range(3) for _ in range(chunks)]
    out_specs = [column(0)] * (2 * chunks) + [
        pl.BlockSpec((1, 8, total), lambda j, k, o: (2 * j + k, 0, 0))
    ]
    outs = pl.pallas_call(
        functools.partial(attn_forward_kernel, chunks, total // BLOCK),
        grid_spec=pltpu.PrefetchScalarGridSpec(
            num_scalar_prefetch=1,
            grid=(pairs, 2),
            in_specs=row_specs + [pl.BlockSpec((1, LANES), lambda j, k, o: (0, j))],
            out_specs=out_specs,
            scratch_shapes=[pltpu.VMEM((total, LANES), BF16)] * 3
            + [pltpu.VMEM((total, LANES), F32)],
        ),
        out_shape=[jax.ShapeDtypeStruct((rows, width), BF16)] * (2 * chunks)
        + [jax.ShapeDtypeStruct((2 * pairs, 8, total), F32)],
        compiler_params=pltpu.CompilerParams(
            dimension_semantics=("arbitrary", "arbitrary"), vmem_limit_bytes=48 << 20
        ),
        name="attn_forward",
    )(offs, *[part for _ in range(3) for part in projected], columns)
    return outs[:chunks], outs[chunks : 2 * chunks], outs[-1]


def attn_backward_kernel(chunks, blocks, offs, *refs):
    groups = [refs[t * chunks : (t + 1) * chunks] for t in range(5)]
    lse_ref = refs[5 * chunks]
    rest = refs[5 * chunks + 1 :]
    grad_out = rest[:chunks]
    qb, kb, vb, gb, delta, dq, dk, dv = rest[chunks:]
    pair, parity = pl.program_id(0), pl.program_id(1)
    rows = groups[0][0].shape[0]
    width = pl.num_programs(0) * LANES
    lane_head = lax.broadcasted_iota(jnp.int32, (BLOCK, LANES), 1) // HD
    mine = lane_head == parity

    @pl.when(parity == 0)
    def _():
        for t in range(chunks):
            start = pl.multiple_of(offs[t], BLOCK)
            place = pl.ds(start, rows)
            for buf, group in zip((qb, kb, vb, gb), groups):
                buf[place, :] = group[t][...]
            for i in range(rows // BLOCK):
                here = slice(i * BLOCK, (i + 1) * BLOCK)
                product = groups[3][t][here, :].astype(F32) * groups[4][t][here, :].astype(F32)
                turned = product.T
                there = pl.ds(pl.multiple_of(start + i * BLOCK, BLOCK), BLOCK)
                for head in range(2):
                    part = turned[head * HD : (head + 1) * HD, :]
                    delta[head, :, there] = jnp.broadcast_to(
                        jnp.sum(part, axis=0, keepdims=True), (8, BLOCK)
                    )
        dk[...] = jnp.zeros_like(dk)
        dv[...] = jnp.zeros_like(dv)

    for i in range(blocks):
        here = slice(i * BLOCK, (i + 1) * BLOCK)
        keys = slice(0, (i + 1) * BLOCK)
        q = jnp.where(mine, qb[here, :] * BF16(HD**-0.5), BF16(0))
        grad = jnp.where(mine, gb[here, :], BF16(0))
        scores = dot(kb[keys, :], q, ((1,), (1,)))
        probs = jnp.exp(scores - lse_ref[0, 0:1, here])
        grad_probs = dot(vb[keys, :], grad, ((1,), (1,)))
        grad_scores = (probs * (grad_probs - delta[parity, 0:1, here])).astype(BF16)
        dv[keys, :] += dot(probs.astype(BF16), grad)
        dk[keys, :] += dot(grad_scores, q)
        grad_q = dot(grad_scores, kb[keys, :], ((0,), (0,))) * HD**-0.5
        dq[here, :] = jnp.where(mine, grad_q, dq[here, :])

    @pl.when(parity == 1)
    def _():
        for t in range(chunks):
            place = pl.ds(pl.multiple_of(offs[t], BLOCK), rows)
            for n, buf in enumerate((dq, dk, dv)):
                where = pl.ds(pl.multiple_of(n * width + pair * LANES, LANES), LANES)
                grad_out[t][:, where] = buf[place, :].astype(BF16)


def attn_backward(offs, projected, grad_attended, attended, lse):
    chunks = len(projected)
    rows, width = projected[0].shape[0], projected[0].shape[1] // 3
    total, pairs = rows * chunks, width // LANES

    def column(t):
        return pl.BlockSpec((rows, LANES), lambda j, k, o: (0, t * pairs + j))

    in_specs = [column(t) for t in (0, 1, 2, 0, 0) for _ in range(chunks)]
    return pl.pallas_call(
        functools.partial(attn_backward_kernel, chunks, total // BLOCK),
        grid_spec=pltpu.PrefetchScalarGridSpec(
            num_scalar_prefetch=1,
            grid=(pairs, 2),
            in_specs=in_specs
            + [pl.BlockSpec((1, 8, total), lambda j, k, o: (2 * j + k, 0, 0))],
            out_specs=[pl.BlockSpec((rows, 3 * width), lambda j, k, o: (0, 0))] * chunks,
            scratch_shapes=[pltpu.VMEM((total, LANES), BF16)] * 4
            + [pltpu.VMEM((2, 8, total), F32)]
            + [pltpu.VMEM((total, LANES), F32)] * 3,
        ),
        out_shape=[jax.ShapeDtypeStruct((rows, 3 * width), BF16)] * chunks,
        compiler_params=pltpu.CompilerParams(
            dimension_semantics=("arbitrary", "arbitrary"), vmem_limit_bytes=56 << 20
        ),
        name="attn_backward",
    )(
        offs,
        *[part for _ in range(3) for part in projected],
        *grad_attended,
        *attended,
        lse,
    )


def exchange(a):
    return lax.ppermute(a, ("c", "h"), [(0, 0), (1, 2), (2, 1), (3, 3)])


def other_core(a):
    return lax.ppermute(a, "c", [(0, 1), (1, 0)])


def normalize(row_values):
    row_mean = jnp.mean(row_values, axis=-1, keepdims=True)
    centred = row_values - row_mean
    spread = jnp.mean(centred * centred, axis=-1, keepdims=True)
    inverse = lax.rsqrt(spread + NORM_EPS)
    return (centred * inverse, inverse)


def norm_back(gradient, normed, inverse):
    return inverse * (
        gradient
        - jnp.mean(gradient, axis=-1, keepdims=True)
        - normed * jnp.mean(gradient * normed, axis=-1, keepdims=True)
    )


def body(
    paired,
    tokens,
    w_qkv,
    w_out,
    w_in,
    w_back,
    gain_attn,
    gain_post,
    gain_ffn,
    gain_mid,
    head_scale,
    cotangent,
):
    def spread_tokens(a):
        if paired:
            return [a, other_core(a)]
        return [lax.all_gather(a, PART_AXES, axis=0, tiled=True)]

    def collect_tokens(make):
        if paired:
            sent = other_core(make(1).astype(BF16))
            return make(0) + sent.astype(F32)
        return lax.psum_scatter(
            make(0).astype(BF16), PART_AXES, scatter_dimension=0, tiled=True
        ).astype(F32)

    def sum_parts(values):
        if paired:
            theirs = other_core(jnp.stack(values))
            return [values[0] + theirs[1], values[1] + theirs[0]]
        return [lax.psum(values[0], PART_AXES)]

    def weight_grad(left, right):
        total = sum(dot(a, b, ((0,), (0,))) for a, b in zip(left, right))
        return lax.psum_scatter(
            total.astype(BF16), WEIGHT_AXES, scatter_dimension=0, tiled=True
        )

    core = lax.axis_index("c")
    ranks = lax.axis_size("p") * lax.axis_size("h")
    depth, _, feat_width = w_qkv.shape
    model = depth * ranks
    parts = 2 if paired else 1

    small = jnp.concatenate([gain_attn, gain_post, gain_ffn, gain_mid])
    columns = -(-small.shape[0] // depth)
    small = jnp.pad(small, (0, columns * depth - small.shape[0])).reshape(depth, columns)
    small = jnp.pad(small, ((0, 0), (0, LANES - columns)))
    first = jnp.concatenate([w_qkv.reshape(depth, 3 * feat_width), small], axis=1)
    first, tokens, scale, w_out_own, w_in_own, w_back_own = (
        exchange(first),
        exchange(tokens),
        exchange(head_scale),
        exchange(w_out),
        exchange(w_in),
        exchange(w_back),
    )

    def gather(a):
        return lax.all_gather(a, WEIGHT_AXES, axis=0, tiled=True)

    first = gather(first)
    w_mix, w_up, w_down = gather(w_out_own), gather(w_in_own), gather(w_back_own)
    w_proj = first[:, : 3 * feat_width]
    small = first[:, 3 * feat_width : 3 * feat_width + columns].astype(F32)
    small = small.reshape(ranks, depth * columns)
    mid_rows = gain_mid.shape[0]
    g_attn, g_post, g_ffn = (
        small[:, n * depth : (n + 1) * depth].reshape(1, model) for n in range(3)
    )
    g_mid = small[:, 3 * depth : 3 * depth + mid_rows].reshape(1, ranks * mid_rows)
    hidden = ranks * mid_rows * lax.axis_size(PART_AXES)

    inputs = tokens.astype(F32)
    rows = inputs.shape[0]
    if paired:
        offs = jnp.stack([core * rows, (1 - core) * rows]).astype(jnp.int32)
    else:
        offs = jnp.zeros((1,), jnp.int32)
    column_scale = jnp.repeat(scale.astype(F32), HD)[None, :]

    norm_attn, inv_attn = normalize(inputs)
    gathered = spread_tokens((norm_attn * g_attn).astype(BF16))
    projected = [dot(part, w_proj).astype(BF16) for part in gathered]
    attended, scaled, lse = attn_forward(offs, projected, column_scale)
    mixed_sum = collect_tokens(lambda t: dot(scaled[t], w_mix))
    norm_post, inv_post = normalize(mixed_sum)
    middle = inputs + norm_post * g_post
    norm_ffn, inv_ffn = normalize(middle)
    gathered_ffn = spread_tokens((norm_ffn * g_ffn).astype(BF16))
    upper = [dot(part, w_up) for part in gathered_ffn]
    active = [jax.nn.gelu(u, approximate=False) for u in upper]
    sums = sum_parts(
        [jnp.stack([jnp.sum(a, axis=-1), jnp.sum(a * a, axis=-1)]) for a in active]
    )
    mean_mid = [s[0][:, None] / hidden for s in sums]
    inv_mid = [
        lax.rsqrt(s[1][:, None] / hidden - m * m + NORM_EPS) for s, m in zip(sums, mean_mid)
    ]
    norm_mid = [(a - m) * r for a, m, r in zip(active, mean_mid, inv_mid)]
    fed_down = [(n * g_mid).astype(BF16) for n in norm_mid]
    output = middle + collect_tokens(lambda t: dot(fed_down[t], w_down))
    output = exchange(output.astype(BF16))

    cotangent = exchange(cotangent)
    grad_top = cotangent.astype(F32)
    grad_full = spread_tokens(cotangent)
    grad_down = weight_grad(fed_down, grad_full)
    grad_fed = [dot(g, w_down, ((1,), (1,))) for g in grad_full]
    grad_gmid = sum(jnp.sum(g * n, axis=0) for g, n in zip(grad_fed, norm_mid))
    scaled_mid = [g * g_mid for g in grad_fed]
    moments = sum_parts(
        [
            jnp.stack([jnp.sum(g, axis=-1), jnp.sum(g * n, axis=-1)])
            for g, n in zip(scaled_mid, norm_mid)
        ]
    )
    grad_upper = []
    for t in range(parts):
        grad_active = inv_mid[t] * (
            scaled_mid[t]
            - moments[t][0][:, None] / hidden
            - norm_mid[t] * (moments[t][1][:, None] / hidden)
        )
        u = upper[t]
        normal_cdf = 0.5 * (1.0 + lax.erf(u * 0.7071067811865476))
        density = jnp.exp(-0.5 * u * u) * 0.3989422804014327
        grad_upper.append((grad_active * (normal_cdf + u * density)).astype(BF16))
    grad_up = weight_grad(gathered_ffn, grad_upper)
    grad_entry_ffn = collect_tokens(lambda t: dot(grad_upper[t], w_up, ((1,), (1,))))
    grad_gffn = jnp.sum(grad_entry_ffn * norm_ffn, axis=0)
    grad_middle = grad_top + norm_back(grad_entry_ffn * g_ffn, norm_ffn, inv_ffn)
    grad_gpost = jnp.sum(grad_middle * norm_post, axis=0)
    grad_mixed = norm_back(grad_middle * g_post, norm_post, inv_post).astype(BF16)
    grad_mfull = spread_tokens(grad_mixed)
    grad_mix = weight_grad(scaled, grad_mfull)
    grad_scaled = [dot(g, w_mix, ((1,), (1,))) for g in grad_mfull]
    grad_heads = sum(
        jnp.sum(jnp.sum(g * a.astype(F32), axis=0).reshape(-1, HD), axis=1)
        for g, a in zip(grad_scaled, attended)
    )
    grad_attended = [(g * column_scale).astype(BF16) for g in grad_scaled]
    grad_proj = attn_backward(offs, projected, grad_attended, attended, lse)
    grad_wproj = weight_grad(gathered, grad_proj)
    grad_entry_attn = collect_tokens(lambda t: dot(grad_proj[t], w_proj, ((1,), (1,))))
    grad_gattn = jnp.sum(grad_entry_attn * norm_attn, axis=0)
    grad_inputs = grad_middle + norm_back(grad_entry_attn * g_attn, norm_attn, inv_attn)
    grad_inputs = exchange(grad_inputs.astype(BF16))

    slot = lax.axis_index(PART_AXES)
    slots = lax.axis_size(PART_AXES)
    own = jnp.concatenate([grad_gmid, grad_heads])
    placed = jnp.where(jnp.arange(slots)[:, None] == slot, own[None, :], 0.0).reshape(-1)
    sums = lax.psum(jnp.concatenate([grad_gattn, grad_gpost, grad_gffn, placed]), ALL_AXES)
    device_dp = lax.axis_index(("p", "c"))
    device_mp = lax.axis_index(("h", "l"))
    short = depth // slots
    starts = device_dp * depth + device_mp * short
    gains = [
        lax.dynamic_slice_in_dim(sums, n * model + starts, short) for n in range(3)
    ]
    base = 3 * model + device_mp * own.shape[0]
    grad_mid = lax.dynamic_slice_in_dim(sums, base + device_dp * mid_rows, mid_rows)
    grad_scale = lax.dynamic_slice_in_dim(
        sums, base + grad_gmid.shape[0], grad_heads.shape[0]
    )
    return (
        output,
        grad_inputs,
        exchange(grad_wproj).astype(F32).reshape(depth, 3, feat_width),
        exchange(grad_mix).astype(F32),
        exchange(grad_up).astype(F32),
        exchange(grad_down).astype(F32),
        *gains,
        grad_mid,
        grad_scale,
    )


def solution(mesh):
    data, split = mesh.shape["dp"], mesh.shape["mp"]
    named = Mesh(mesh.devices.reshape(data // 2, 2, 2, split // 2), ALL_AXES)
    dp, mp = ("p", "c"), ("h", "l")
    specs = (
        P(dp + mp, None),
        P(dp, None, mp),
        P(mp + dp, None),
        P(dp, mp),
        P(mp + dp, None),
    )
    return jax.shard_map(
        functools.partial(body, split == 2),
        mesh=named,
        in_specs=specs + (P(dp), P(dp), P(dp), P(mp + dp), P(mp), P(dp + mp, None)),
        out_specs=specs[:1]
        + specs
        + (P(dp + mp), P(dp + mp), P(dp + mp), P(mp + dp), P(mp)),
        check_vma=False,
    )
```

```python
import functools

import jax
import jax.numpy as jnp
from jax import lax
from jax.experimental import pallas as pl
from jax.experimental.pallas import tpu as pltpu
from jax.sharding import Mesh, PartitionSpec as P

HD = 64
BLOCK = 256
LANES = 128
NORM_EPS = 1e-05
F32 = jnp.float32
BF16 = jnp.bfloat16
WEIGHT_AXES = ("p", "h")
PART_AXES = ("c", "l")
ALL_AXES = ("p", "c", "h", "l")


def dot(a, b, dims=((1,), (0,))):
    return lax.dot_general(a, b, (dims, ((), ())), preferred_element_type=F32)


def attn_forward_kernel(chunks, blocks, offs, *refs):
    q_in, k_in, v_in = (refs[t * chunks : (t + 1) * chunks] for t in range(3))
    scale_ref = refs[3 * chunks]
    rest = refs[3 * chunks + 1 :]
    att_out, scaled_out = rest[:chunks], rest[chunks : 2 * chunks]
    lse_ref, qb, kb, vb, ob = rest[2 * chunks :]
    parity = pl.program_id(1)
    rows = q_in[0].shape[0]

    @pl.when(parity == 0)
    def _():
        for t in range(chunks):
            place = pl.ds(pl.multiple_of(offs[t], BLOCK), rows)
            qb[place, :] = q_in[t][...]
            kb[place, :] = k_in[t][...]
            vb[place, :] = v_in[t][...]

    lane_head = lax.broadcasted_iota(jnp.int32, (BLOCK, LANES), 1) // HD
    mine = lane_head == parity
    for i in range(blocks):
        here = slice(i * BLOCK, (i + 1) * BLOCK)
        keys = slice(0, (i + 1) * BLOCK)
        q = jnp.where(mine, qb[here, :] * BF16(HD**-0.5), BF16(0))
        scores = dot(q, kb[keys, :], ((1,), (1,)))
        top = jnp.max(scores, axis=1, keepdims=True)
        weights = jnp.exp(scores - top)
        total = jnp.sum(weights, axis=1, keepdims=True)
        out = dot(weights.astype(BF16), vb[keys, :]) / total
        lse = jnp.broadcast_to(top + jnp.log(total), (BLOCK, LANES))
        lse_ref[0, :, here] = lse.T[:8, :]
        ob[here, :] = jnp.where(mine, out, ob[here, :])

    @pl.when(parity == 1)
    def _():
        for t in range(chunks):
            place = pl.ds(pl.multiple_of(offs[t], BLOCK), rows)
            out = ob[place, :]
            att_out[t][...] = out.astype(BF16)
            scaled_out[t][...] = (out * scale_ref[...]).astype(BF16)


def attn_forward(offs, projected, columns):
    chunks = len(projected)
    rows, width = projected[0].shape[0], projected[0].shape[1] // 3
    total, pairs = rows * chunks, width // LANES

    def column(t):
        return pl.BlockSpec((rows, LANES), lambda j, k, o: (0, t * pairs + j))

    row_specs = [column(t) for t in range(3) for _ in range(chunks)]
    out_specs = [column(0)] * (2 * chunks) + [
        pl.BlockSpec((1, 8, total), lambda j, k, o: (2 * j + k, 0, 0))
    ]
    outs = pl.pallas_call(
        functools.partial(attn_forward_kernel, chunks, total // BLOCK),
        grid_spec=pltpu.PrefetchScalarGridSpec(
            num_scalar_prefetch=1,
            grid=(pairs, 2),
            in_specs=row_specs + [pl.BlockSpec((1, LANES), lambda j, k, o: (0, j))],
            out_specs=out_specs,
            scratch_shapes=[pltpu.VMEM((total, LANES), BF16)] * 3
            + [pltpu.VMEM((total, LANES), F32)],
        ),
        out_shape=[jax.ShapeDtypeStruct((rows, width), BF16)] * (2 * chunks)
        + [jax.ShapeDtypeStruct((2 * pairs, 8, total), F32)],
        compiler_params=pltpu.CompilerParams(
            dimension_semantics=("arbitrary", "arbitrary"), vmem_limit_bytes=48 << 20
        ),
        name="attn_forward",
    )(offs, *[part for _ in range(3) for part in projected], columns)
    return outs[:chunks], outs[chunks : 2 * chunks], outs[-1]


def attn_backward_kernel(chunks, blocks, offs, *refs):
    groups = [refs[t * chunks : (t + 1) * chunks] for t in range(5)]
    lse_ref = refs[5 * chunks]
    rest = refs[5 * chunks + 1 :]
    grad_out = rest[:chunks]
    qb, kb, vb, gb, delta, dq, dk, dv = rest[chunks:]
    pair, parity = pl.program_id(0), pl.program_id(1)
    rows = groups[0][0].shape[0]
    width = pl.num_programs(0) * LANES
    lane_head = lax.broadcasted_iota(jnp.int32, (BLOCK, LANES), 1) // HD
    mine = lane_head == parity

    @pl.when(parity == 0)
    def _():
        for t in range(chunks):
            start = pl.multiple_of(offs[t], BLOCK)
            place = pl.ds(start, rows)
            for buf, group in zip((qb, kb, vb, gb), groups):
                buf[place, :] = group[t][...]
            for i in range(rows // BLOCK):
                here = slice(i * BLOCK, (i + 1) * BLOCK)
                product = groups[3][t][here, :].astype(F32) * groups[4][t][here, :].astype(F32)
                turned = product.T
                there = pl.ds(pl.multiple_of(start + i * BLOCK, BLOCK), BLOCK)
                for head in range(2):
                    part = turned[head * HD : (head + 1) * HD, :]
                    delta[head, :, there] = jnp.broadcast_to(
                        jnp.sum(part, axis=0, keepdims=True), (8, BLOCK)
                    )
        dk[...] = jnp.zeros_like(dk)
        dv[...] = jnp.zeros_like(dv)

    for i in range(blocks):
        here = slice(i * BLOCK, (i + 1) * BLOCK)
        keys = slice(0, (i + 1) * BLOCK)
        q = jnp.where(mine, qb[here, :] * BF16(HD**-0.5), BF16(0))
        grad = jnp.where(mine, gb[here, :], BF16(0))
        scores = dot(kb[keys, :], q, ((1,), (1,)))
        probs = jnp.exp(scores - lse_ref[0, 0:1, here])
        grad_probs = dot(vb[keys, :], grad, ((1,), (1,)))
        grad_scores = (probs * (grad_probs - delta[parity, 0:1, here])).astype(BF16)
        dv[keys, :] += dot(probs.astype(BF16), grad)
        dk[keys, :] += dot(grad_scores, q)
        grad_q = dot(grad_scores, kb[keys, :], ((0,), (0,))) * HD**-0.5
        dq[here, :] = jnp.where(mine, grad_q, dq[here, :])

    @pl.when(parity == 1)
    def _():
        for t in range(chunks):
            place = pl.ds(pl.multiple_of(offs[t], BLOCK), rows)
            for n, buf in enumerate((dq, dk, dv)):
                where = pl.ds(pl.multiple_of(n * width + pair * LANES, LANES), LANES)
                grad_out[t][:, where] = buf[place, :].astype(BF16)


def attn_backward(offs, projected, grad_attended, attended, lse):
    chunks = len(projected)
    rows, width = projected[0].shape[0], projected[0].shape[1] // 3
    total, pairs = rows * chunks, width // LANES

    def column(t):
        return pl.BlockSpec((rows, LANES), lambda j, k, o: (0, t * pairs + j))

    in_specs = [column(t) for t in (0, 1, 2, 0, 0) for _ in range(chunks)]
    return pl.pallas_call(
        functools.partial(attn_backward_kernel, chunks, total // BLOCK),
        grid_spec=pltpu.PrefetchScalarGridSpec(
            num_scalar_prefetch=1,
            grid=(pairs, 2),
            in_specs=in_specs
            + [pl.BlockSpec((1, 8, total), lambda j, k, o: (2 * j + k, 0, 0))],
            out_specs=[pl.BlockSpec((rows, 3 * width), lambda j, k, o: (0, 0))] * chunks,
            scratch_shapes=[pltpu.VMEM((total, LANES), BF16)] * 4
            + [pltpu.VMEM((2, 8, total), F32)]
            + [pltpu.VMEM((total, LANES), F32)] * 3,
        ),
        out_shape=[jax.ShapeDtypeStruct((rows, 3 * width), BF16)] * chunks,
        compiler_params=pltpu.CompilerParams(
            dimension_semantics=("arbitrary", "arbitrary"), vmem_limit_bytes=56 << 20
        ),
        name="attn_backward",
    )(
        offs,
        *[part for _ in range(3) for part in projected],
        *grad_attended,
        *attended,
        lse,
    )


def exchange(a):
    return lax.ppermute(a, ("c", "h"), [(0, 0), (1, 2), (2, 1), (3, 3)])


def other_core(a):
    return lax.ppermute(a, "c", [(0, 1), (1, 0)])


def rank_pairs(ranks, bit):
    return [(r, r ^ (1 << bit)) for r in range(ranks)]


def halving_sum(total, ranks, order):
    rank = lax.axis_index(WEIGHT_AXES)
    rows, columns = total.shape[0] // ranks, total.shape[1]
    left = list(range(ranks.bit_length() - 1))
    for bit in order:
        low = 1 << left.index(bit)
        left.remove(bit)
        view = total.reshape(-1, 2, low * rows, columns)
        mine = (rank >> bit) & 1
        sent = lax.dynamic_index_in_dim(view, 1 - mine, 1, keepdims=False)
        kept = lax.dynamic_index_in_dim(view, mine, 1, keepdims=False)
        theirs = lax.ppermute(sent.astype(BF16), WEIGHT_AXES, rank_pairs(ranks, bit))
        total = kept.astype(F32) + theirs.astype(F32)
        if left:
            total = total.astype(BF16)
        total = total.reshape(-1, columns)
    return total


def doubling_sum(values, ranks):
    for bit in range(ranks.bit_length() - 1):
        values = values + lax.ppermute(values, WEIGHT_AXES, rank_pairs(ranks, bit))
    return values


def normalize(row_values):
    row_mean = jnp.mean(row_values, axis=-1, keepdims=True)
    centred = row_values - row_mean
    spread = jnp.mean(centred * centred, axis=-1, keepdims=True)
    inverse = lax.rsqrt(spread + NORM_EPS)
    return (centred * inverse, inverse)


def norm_back(gradient, normed, inverse):
    return inverse * (
        gradient
        - jnp.mean(gradient, axis=-1, keepdims=True)
        - normed * jnp.mean(gradient * normed, axis=-1, keepdims=True)
    )


def body(
    paired,
    tokens,
    w_qkv,
    w_out,
    w_in,
    w_back,
    gain_attn,
    gain_post,
    gain_ffn,
    gain_mid,
    head_scale,
    cotangent,
):
    def spread_tokens(a):
        if paired:
            return [a, other_core(a)]
        return [lax.all_gather(a, PART_AXES, axis=0, tiled=True)]

    def collect_tokens(make):
        if paired:
            sent = other_core(make(1).astype(BF16))
            return make(0) + sent.astype(F32)
        return lax.psum_scatter(
            make(0).astype(BF16), PART_AXES, scatter_dimension=0, tiled=True
        ).astype(F32)

    def sum_parts(values):
        if paired:
            theirs = other_core(jnp.stack(values))
            return [values[0] + theirs[1], values[1] + theirs[0]]
        return [lax.psum(values[0], PART_AXES)]

    def product(left, right):
        return sum(dot(a, b, ((0,), (0,))) for a, b in zip(left, right)).astype(BF16)

    def scatter(total):
        return lax.psum_scatter(total, WEIGHT_AXES, scatter_dimension=0, tiled=True)

    def scatter_fast(total, splits):
        bits = list(range(ranks.bit_length() - 1))
        orders = [bits, [bits[1], bits[0]] + bits[2:]]
        width = total.shape[1] // splits
        pieces = [
            halving_sum(total[:, n * width : (n + 1) * width], ranks, orders[n % 2])
            for n in range(splits)
        ]
        return pieces[0] if splits == 1 else jnp.concatenate(pieces, axis=1)

    core = lax.axis_index("c")
    ranks = lax.axis_size("p") * lax.axis_size("h")
    depth, _, feat_width = w_qkv.shape
    model = depth * ranks
    parts = 2 if paired else 1

    small = jnp.concatenate([gain_attn, gain_post, gain_ffn, gain_mid])
    columns = -(-small.shape[0] // depth)
    small = jnp.pad(small, (0, columns * depth - small.shape[0])).reshape(depth, columns)
    small = jnp.pad(small, ((0, 0), (0, LANES - columns)))
    first = jnp.concatenate([w_qkv.reshape(depth, 3 * feat_width), small], axis=1)
    first, tokens, scale, w_out_own, w_in_own, w_back_own = (
        exchange(first),
        exchange(tokens),
        exchange(head_scale),
        exchange(w_out),
        exchange(w_in),
        exchange(w_back),
    )

    def gather(a):
        return lax.all_gather(a, WEIGHT_AXES, axis=0, tiled=True)

    first = gather(first)
    w_mix, w_up, w_down = gather(w_out_own), gather(w_in_own), gather(w_back_own)
    w_proj = first[:, : 3 * feat_width]
    small = first[:, 3 * feat_width : 3 * feat_width + columns].astype(F32)
    small = small.reshape(ranks, depth * columns)
    mid_rows = gain_mid.shape[0]
    g_attn, g_post, g_ffn = (
        small[:, n * depth : (n + 1) * depth].reshape(1, model) for n in range(3)
    )
    g_mid = small[:, 3 * depth : 3 * depth + mid_rows].reshape(1, ranks * mid_rows)
    hidden = ranks * mid_rows * lax.axis_size(PART_AXES)

    inputs = tokens.astype(F32)
    rows = inputs.shape[0]
    if paired:
        offs = jnp.stack([core * rows, (1 - core) * rows]).astype(jnp.int32)
    else:
        offs = jnp.zeros((1,), jnp.int32)
    column_scale = jnp.repeat(scale.astype(F32), HD)[None, :]

    norm_attn, inv_attn = normalize(inputs)
    gathered = spread_tokens((norm_attn * g_attn).astype(BF16))
    projected = [dot(part, w_proj).astype(BF16) for part in gathered]
    attended, scaled, lse = attn_forward(offs, projected, column_scale)
    mixed_sum = collect_tokens(lambda t: dot(scaled[t], w_mix))
    norm_post, inv_post = normalize(mixed_sum)
    middle = inputs + norm_post * g_post
    norm_ffn, inv_ffn = normalize(middle)
    gathered_ffn = spread_tokens((norm_ffn * g_ffn).astype(BF16))
    upper = [dot(part, w_up) for part in gathered_ffn]
    active = [jax.nn.gelu(u, approximate=False) for u in upper]
    sums = sum_parts(
        [jnp.stack([jnp.sum(a, axis=-1), jnp.sum(a * a, axis=-1)]) for a in active]
    )
    mean_mid = [s[0][:, None] / hidden for s in sums]
    inv_mid = [
        lax.rsqrt(s[1][:, None] / hidden - m * m + NORM_EPS) for s, m in zip(sums, mean_mid)
    ]
    norm_mid = [(a - m) * r for a, m, r in zip(active, mean_mid, inv_mid)]
    fed_down = [(n * g_mid).astype(BF16) for n in norm_mid]
    output = middle + collect_tokens(lambda t: dot(fed_down[t], w_down))
    output = exchange(output.astype(BF16))

    cotangent = exchange(cotangent)
    grad_top = cotangent.astype(F32)
    grad_full = spread_tokens(cotangent)
    grad_down = product(fed_down, grad_full)
    grad_down, grad_full = lax.optimization_barrier((grad_down, grad_full))
    grad_down = scatter(grad_down)
    grad_fed = [dot(g, w_down, ((1,), (1,))) for g in grad_full]
    grad_gmid = sum(jnp.sum(g * n, axis=0) for g, n in zip(grad_fed, norm_mid))
    scaled_mid = [g * g_mid for g in grad_fed]
    moments = sum_parts(
        [
            jnp.stack([jnp.sum(g, axis=-1), jnp.sum(g * n, axis=-1)])
            for g, n in zip(scaled_mid, norm_mid)
        ]
    )
    grad_upper = []
    for t in range(parts):
        grad_active = inv_mid[t] * (
            scaled_mid[t]
            - moments[t][0][:, None] / hidden
            - norm_mid[t] * (moments[t][1][:, None] / hidden)
        )
        u = upper[t]
        normal_cdf = 0.5 * (1.0 + lax.erf(u * 0.7071067811865476))
        density = jnp.exp(-0.5 * u * u) * 0.3989422804014327
        grad_upper.append((grad_active * (normal_cdf + u * density)).astype(BF16))
    grad_up = scatter(product(gathered_ffn, grad_upper))
    grad_entry_ffn = collect_tokens(lambda t: dot(grad_upper[t], w_up, ((1,), (1,))))
    grad_gffn = jnp.sum(grad_entry_ffn * norm_ffn, axis=0)
    grad_middle = grad_top + norm_back(grad_entry_ffn * g_ffn, norm_ffn, inv_ffn)
    grad_gpost = jnp.sum(grad_middle * norm_post, axis=0)
    grad_mixed = norm_back(grad_middle * g_post, norm_post, inv_post).astype(BF16)
    grad_mfull = spread_tokens(grad_mixed)
    grad_mix = scatter_fast(product(scaled, grad_mfull), 1)
    grad_scaled = [dot(g, w_mix, ((1,), (1,))) for g in grad_mfull]
    grad_heads = sum(
        jnp.sum(jnp.sum(g * a.astype(F32), axis=0).reshape(-1, HD), axis=1)
        for g, a in zip(grad_scaled, attended)
    )
    grad_attended = [(g * column_scale).astype(BF16) for g in grad_scaled]
    grad_proj = attn_backward(offs, projected, grad_attended, attended, lse)
    grad_wproj = scatter_fast(product(gathered, grad_proj), 2)
    grad_entry_attn = collect_tokens(lambda t: dot(grad_proj[t], w_proj, ((1,), (1,))))
    grad_gattn = jnp.sum(grad_entry_attn * norm_attn, axis=0)
    grad_inputs = grad_middle + norm_back(grad_entry_attn * g_attn, norm_attn, inv_attn)
    grad_inputs = exchange(grad_inputs.astype(BF16))

    gains = jnp.concatenate([grad_gattn, grad_gpost, grad_gffn])
    own = doubling_sum(jnp.concatenate([gains, grad_gmid, grad_heads]), ranks)
    device_dp = lax.axis_index(("p", "c"))
    device_mp = lax.axis_index(("h", "l"))
    if paired:
        theirs = other_core(own)
        gains = own[: 3 * model] + theirs[: 3 * model]
        own = jnp.where(core == lax.axis_index("h"), own, theirs)[3 * model :]
    else:
        gains = lax.psum(own[: 3 * model], PART_AXES)
        own = exchange(own[3 * model :])
    short = depth // lax.axis_size(PART_AXES)
    starts = device_dp * depth + device_mp * short
    gains = [
        lax.dynamic_slice_in_dim(gains, n * model + starts, short) for n in range(3)
    ]
    grad_mid = lax.dynamic_slice_in_dim(own, device_dp * mid_rows, mid_rows)
    grad_scale = own[grad_gmid.shape[0] :]
    return (
        output,
        grad_inputs,
        exchange(grad_wproj.astype(BF16)).astype(F32).reshape(depth, 3, feat_width),
        exchange(grad_mix.astype(BF16)).astype(F32),
        exchange(grad_up).astype(F32),
        exchange(grad_down).astype(F32),
        *gains,
        grad_mid,
        grad_scale,
    )


def solution(mesh):
    data, split = mesh.shape["dp"], mesh.shape["mp"]
    named = Mesh(mesh.devices.reshape(data // 2, 2, 2, split // 2), ALL_AXES)
    dp, mp = ("p", "c"), ("h", "l")
    specs = (
        P(dp + mp, None),
        P(dp, None, mp),
        P(mp + dp, None),
        P(dp, mp),
        P(mp + dp, None),
    )
    return jax.shard_map(
        functools.partial(body, split == 2),
        mesh=named,
        in_specs=specs + (P(dp), P(dp), P(dp), P(mp + dp), P(mp), P(dp + mp, None)),
        out_specs=specs[:1]
        + specs
        + (P(dp + mp), P(dp + mp), P(dp + mp), P(mp + dp), P(mp)),
        check_vma=False,
    )
```

```python
import functools

import jax
import jax.numpy as jnp
from jax import lax
from jax.experimental import pallas as pl
from jax.experimental.pallas import tpu as pltpu
from jax.sharding import Mesh, PartitionSpec as P

HD = 64
BLOCK = 256
LANES = 128
NORM_EPS = 1e-05
F32 = jnp.float32
BF16 = jnp.bfloat16
WEIGHT_AXES = ("p", "h")
PART_AXES = ("c", "l")
ALL_AXES = ("p", "c", "h", "l")


def dot(a, b, dims=((1,), (0,))):
    return lax.dot_general(a, b, (dims, ((), ())), preferred_element_type=F32)


def attn_forward_kernel(chunks, blocks, offs, *refs):
    q_in, k_in, v_in = (refs[t * chunks : (t + 1) * chunks] for t in range(3))
    scale_ref = refs[3 * chunks]
    rest = refs[3 * chunks + 1 :]
    att_out, scaled_out = rest[:chunks], rest[chunks : 2 * chunks]
    lse_ref, qb, kb, vb, ob = rest[2 * chunks :]
    parity = pl.program_id(1)
    rows = q_in[0].shape[0]

    @pl.when(parity == 0)
    def _():
        for t in range(chunks):
            place = pl.ds(pl.multiple_of(offs[t], BLOCK), rows)
            qb[place, :] = q_in[t][...]
            kb[place, :] = k_in[t][...]
            vb[place, :] = v_in[t][...]

    lane_head = lax.broadcasted_iota(jnp.int32, (BLOCK, LANES), 1) // HD
    mine = lane_head == parity
    for i in range(blocks):
        here = slice(i * BLOCK, (i + 1) * BLOCK)
        keys = slice(0, (i + 1) * BLOCK)
        q = jnp.where(mine, qb[here, :] * BF16(HD**-0.5), BF16(0))
        scores = dot(q, kb[keys, :], ((1,), (1,)))
        top = jnp.max(scores, axis=1, keepdims=True)
        weights = jnp.exp(scores - top)
        total = jnp.sum(weights, axis=1, keepdims=True)
        out = dot(weights.astype(BF16), vb[keys, :]) / total
        lse = jnp.broadcast_to(top + jnp.log(total), (BLOCK, LANES))
        lse_ref[0, :, here] = lse.T[:8, :]
        ob[here, :] = jnp.where(mine, out, ob[here, :])

    @pl.when(parity == 1)
    def _():
        for t in range(chunks):
            place = pl.ds(pl.multiple_of(offs[t], BLOCK), rows)
            out = ob[place, :]
            att_out[t][...] = out.astype(BF16)
            scaled_out[t][...] = (out * scale_ref[...]).astype(BF16)


def attn_forward(offs, projected, columns):
    chunks = len(projected)
    rows, width = projected[0].shape[0], projected[0].shape[1] // 3
    total, pairs = rows * chunks, width // LANES

    def column(t):
        return pl.BlockSpec((rows, LANES), lambda j, k, o: (0, t * pairs + j))

    row_specs = [column(t) for t in range(3) for _ in range(chunks)]
    out_specs = [column(0)] * (2 * chunks) + [
        pl.BlockSpec((1, 8, total), lambda j, k, o: (2 * j + k, 0, 0))
    ]
    outs = pl.pallas_call(
        functools.partial(attn_forward_kernel, chunks, total // BLOCK),
        grid_spec=pltpu.PrefetchScalarGridSpec(
            num_scalar_prefetch=1,
            grid=(pairs, 2),
            in_specs=row_specs + [pl.BlockSpec((1, LANES), lambda j, k, o: (0, j))],
            out_specs=out_specs,
            scratch_shapes=[pltpu.VMEM((total, LANES), BF16)] * 3
            + [pltpu.VMEM((total, LANES), F32)],
        ),
        out_shape=[jax.ShapeDtypeStruct((rows, width), BF16)] * (2 * chunks)
        + [jax.ShapeDtypeStruct((2 * pairs, 8, total), F32)],
        compiler_params=pltpu.CompilerParams(
            dimension_semantics=("arbitrary", "arbitrary"), vmem_limit_bytes=48 << 20
        ),
        name="attn_forward",
    )(offs, *[part for _ in range(3) for part in projected], columns)
    return outs[:chunks], outs[chunks : 2 * chunks], outs[-1]


def attn_backward_kernel(chunks, blocks, offs, *refs):
    groups = [refs[t * chunks : (t + 1) * chunks] for t in range(5)]
    lse_ref = refs[5 * chunks]
    rest = refs[5 * chunks + 1 :]
    grad_out = rest[:chunks]
    qb, kb, vb, gb, delta, dq, dk, dv = rest[chunks:]
    pair, parity = pl.program_id(0), pl.program_id(1)
    rows = groups[0][0].shape[0]
    width = pl.num_programs(0) * LANES
    lane_head = lax.broadcasted_iota(jnp.int32, (BLOCK, LANES), 1) // HD
    mine = lane_head == parity

    @pl.when(parity == 0)
    def _():
        for t in range(chunks):
            start = pl.multiple_of(offs[t], BLOCK)
            place = pl.ds(start, rows)
            for buf, group in zip((qb, kb, vb, gb), groups):
                buf[place, :] = group[t][...]
            for i in range(rows // BLOCK):
                here = slice(i * BLOCK, (i + 1) * BLOCK)
                product = groups[3][t][here, :].astype(F32) * groups[4][t][here, :].astype(F32)
                turned = product.T
                there = pl.ds(pl.multiple_of(start + i * BLOCK, BLOCK), BLOCK)
                for head in range(2):
                    part = turned[head * HD : (head + 1) * HD, :]
                    delta[head, :, there] = jnp.broadcast_to(
                        jnp.sum(part, axis=0, keepdims=True), (8, BLOCK)
                    )
        dk[...] = jnp.zeros_like(dk)
        dv[...] = jnp.zeros_like(dv)

    for i in range(blocks):
        here = slice(i * BLOCK, (i + 1) * BLOCK)
        keys = slice(0, (i + 1) * BLOCK)
        q = jnp.where(mine, qb[here, :] * BF16(HD**-0.5), BF16(0))
        grad = jnp.where(mine, gb[here, :], BF16(0))
        scores = dot(kb[keys, :], q, ((1,), (1,)))
        probs = jnp.exp(scores - lse_ref[0, 0:1, here])
        grad_probs = dot(vb[keys, :], grad, ((1,), (1,)))
        grad_scores = (probs * (grad_probs - delta[parity, 0:1, here])).astype(BF16)
        dv[keys, :] += dot(probs.astype(BF16), grad)
        dk[keys, :] += dot(grad_scores, q)
        grad_q = dot(grad_scores, kb[keys, :], ((0,), (0,))) * HD**-0.5
        dq[here, :] = jnp.where(mine, grad_q, dq[here, :])

    @pl.when(parity == 1)
    def _():
        for t in range(chunks):
            place = pl.ds(pl.multiple_of(offs[t], BLOCK), rows)
            for n, buf in enumerate((dq, dk, dv)):
                where = pl.ds(pl.multiple_of(n * width + pair * LANES, LANES), LANES)
                grad_out[t][:, where] = buf[place, :].astype(BF16)


def attn_backward(offs, projected, grad_attended, attended, lse):
    chunks = len(projected)
    rows, width = projected[0].shape[0], projected[0].shape[1] // 3
    total, pairs = rows * chunks, width // LANES

    def column(t):
        return pl.BlockSpec((rows, LANES), lambda j, k, o: (0, t * pairs + j))

    in_specs = [column(t) for t in (0, 1, 2, 0, 0) for _ in range(chunks)]
    return pl.pallas_call(
        functools.partial(attn_backward_kernel, chunks, total // BLOCK),
        grid_spec=pltpu.PrefetchScalarGridSpec(
            num_scalar_prefetch=1,
            grid=(pairs, 2),
            in_specs=in_specs
            + [pl.BlockSpec((1, 8, total), lambda j, k, o: (2 * j + k, 0, 0))],
            out_specs=[pl.BlockSpec((rows, 3 * width), lambda j, k, o: (0, 0))] * chunks,
            scratch_shapes=[pltpu.VMEM((total, LANES), BF16)] * 4
            + [pltpu.VMEM((2, 8, total), F32)]
            + [pltpu.VMEM((total, LANES), F32)] * 3,
        ),
        out_shape=[jax.ShapeDtypeStruct((rows, 3 * width), BF16)] * chunks,
        compiler_params=pltpu.CompilerParams(
            dimension_semantics=("arbitrary", "arbitrary"), vmem_limit_bytes=56 << 20
        ),
        name="attn_backward",
    )(
        offs,
        *[part for _ in range(3) for part in projected],
        *grad_attended,
        *attended,
        lse,
    )


def gelu_parts(u):
    size = jnp.abs(u) * 0.7071067811865476
    t = 1.0 / (1.0 + 0.3275911 * size)
    series = t * (
        0.254829592
        + t * (-0.284496736 + t * (1.421413741 + t * (-1.453152027 + t * 1.061405429)))
    )
    bell = jnp.exp(-size * size)
    tail = 0.5 * series * bell
    cdf = jnp.where(u >= 0, 1.0 - tail, tail)
    return u * cdf, cdf + u * (bell * 0.3989422804014327)


def lane_sum(v):
    return functools.reduce(
        jnp.add, [v[:, n : n + LANES] for n in range(0, v.shape[1], LANES)]
    )


def pack_rows(first, second):
    first = jnp.sum(first, axis=1, keepdims=True)
    second = jnp.sum(second, axis=1, keepdims=True)
    lane = lax.broadcasted_iota(jnp.int32, (first.shape[0], LANES), 1)
    return jnp.where(lane == 0, first, second).T[:8, :]


def unpack_rows(block):
    turned = jnp.concatenate([block] * (LANES // 8), axis=0).T
    return turned[:, 0:1], turned[:, 1:2]


def mid_stats(sums_ref, hidden):
    first, second = unpack_rows(sums_ref[...])
    mean = first / hidden
    return mean, lax.rsqrt(second / hidden - mean * mean + NORM_EPS)


def spans(width, step):
    step = min(step, width)
    return [slice(n, n + step) for n in range(0, width, step)]


def up_kernel(x_ref, w_ref, active_ref, slope_ref, sums_ref):
    x = x_ref[...]
    first = second = 0.0
    for cols in spans(w_ref.shape[1], 512):
        active, slope = gelu_parts(dot(x, w_ref[:, cols]))
        active_ref[:, cols] = active.astype(BF16)
        slope_ref[:, cols] = slope.astype(BF16)
        first += lane_sum(active)
        second += lane_sum(active * active)
    sums_ref[...] = pack_rows(first, second)


def down_kernel(hidden, active_ref, sums_ref, gain_ref, w_ref, fed_ref, out_ref):
    mean, inverse = mid_stats(sums_ref, hidden)
    for cols in spans(active_ref.shape[1], 512):
        normed = (active_ref[:, cols].astype(F32) - mean) * inverse
        fed_ref[:, cols] = (normed * gain_ref[:, cols]).astype(BF16)
    out_ref[...] = dot(fed_ref[...], w_ref[...]).astype(out_ref.dtype)


def down_back_kernel(
    hidden, grad_ref, w_ref, active_ref, sums_ref, gain_ref, back_ref, moments_ref, mid_ref
):
    @pl.when(pl.program_id(0) == 0)
    def _():
        mid_ref[...] = jnp.zeros_like(mid_ref)

    mean, inverse = mid_stats(sums_ref, hidden)
    grad = grad_ref[...]
    first = second = 0.0
    for cols in spans(active_ref.shape[1], 512):
        fed = dot(grad, w_ref[cols, :], ((1,), (1,)))
        normed = (active_ref[:, cols].astype(F32) - mean) * inverse
        along = fed * normed
        mid_ref[:, cols] += jnp.sum(along.reshape(-1, 8, along.shape[1]), axis=0)
        back = fed * gain_ref[:, cols]
        back_ref[:, cols] = back.astype(BF16)
        first += lane_sum(back)
        second += lane_sum(along * gain_ref[:, cols])
    moments_ref[...] = pack_rows(first, second)


def up_back_kernel(
    hidden,
    back_ref,
    active_ref,
    slope_ref,
    sums_ref,
    moments_ref,
    w_ref,
    grad_ref,
    out_ref,
):
    mean, inverse = mid_stats(sums_ref, hidden)
    first, second = unpack_rows(moments_ref[...])
    first, second = first / hidden, second / hidden
    for cols in spans(active_ref.shape[1], 512):
        normed = (active_ref[:, cols].astype(F32) - mean) * inverse
        grad = inverse * (back_ref[:, cols].astype(F32) - first - normed * second)
        grad_ref[:, cols] = (grad * slope_ref[:, cols].astype(F32)).astype(BF16)
    out_ref[...] = dot(grad_ref[...], w_ref[...], ((1,), (1,))).astype(out_ref.dtype)


def row_call(kernel, name, inputs, outputs):
    rows = inputs[0][0].shape[0]
    block = min(BLOCK, rows)

    def spec(shape, how):
        if how == "rows":
            return pl.BlockSpec((block, shape[1]), lambda i: (i, 0))
        if how == "columns":
            return pl.BlockSpec((shape[0], block), lambda i: (0, i))
        return pl.BlockSpec(shape, lambda i: (0, 0))

    return pl.pallas_call(
        kernel,
        grid=(rows // block,),
        in_specs=[spec(a.shape, how) for a, how in inputs],
        out_specs=[spec(shape, how) for shape, _, how in outputs],
        out_shape=[jax.ShapeDtypeStruct(shape, dtype) for shape, dtype, _ in outputs],
        compiler_params=pltpu.CompilerParams(
            dimension_semantics=("arbitrary",), vmem_limit_bytes=48 << 20
        ),
        name=name,
    )(*[a for a, _ in inputs])


def exchange(a):
    return lax.ppermute(a, ("c", "h"), [(0, 0), (1, 2), (2, 1), (3, 3)])


def other_core(a):
    return lax.ppermute(a, "c", [(0, 1), (1, 0)])


def rank_pairs(ranks, bit):
    return [(r, r ^ (1 << bit)) for r in range(ranks)]


def halving_sum(total, ranks, order):
    rank = lax.axis_index(WEIGHT_AXES)
    rows, columns = total.shape[0] // ranks, total.shape[1]
    left = list(range(ranks.bit_length() - 1))
    for bit in order:
        low = 1 << left.index(bit)
        left.remove(bit)
        view = total.reshape(-1, 2, low * rows, columns)
        mine = (rank >> bit) & 1
        sent = lax.dynamic_index_in_dim(view, 1 - mine, 1, keepdims=False)
        kept = lax.dynamic_index_in_dim(view, mine, 1, keepdims=False)
        theirs = lax.ppermute(sent.astype(BF16), WEIGHT_AXES, rank_pairs(ranks, bit))
        total = kept.astype(F32) + theirs.astype(F32)
        if left:
            total = total.astype(BF16)
        total = total.reshape(-1, columns)
    return total


def doubling_sum(values, ranks):
    for bit in range(ranks.bit_length() - 1):
        values = values + lax.ppermute(values, WEIGHT_AXES, rank_pairs(ranks, bit))
    return values


def normalize(row_values):
    row_mean = jnp.mean(row_values, axis=-1, keepdims=True)
    centred = row_values - row_mean
    spread = jnp.mean(centred * centred, axis=-1, keepdims=True)
    inverse = lax.rsqrt(spread + NORM_EPS)
    return (centred * inverse, inverse)


def norm_back(gradient, normed, inverse):
    return inverse * (
        gradient
        - jnp.mean(gradient, axis=-1, keepdims=True)
        - normed * jnp.mean(gradient * normed, axis=-1, keepdims=True)
    )


def body(
    paired,
    tokens,
    w_qkv,
    w_out,
    w_in,
    w_back,
    gain_attn,
    gain_post,
    gain_ffn,
    gain_mid,
    head_scale,
    cotangent,
):
    def spread_tokens(a):
        if paired:
            return [a, other_core(a)]
        return [lax.all_gather(a, PART_AXES, axis=0, tiled=True)]

    def collect_tokens(make):
        if paired:
            sent = other_core(make(1, BF16))
            return make(0, F32) + sent.astype(F32)
        return lax.psum_scatter(
            make(0, BF16), PART_AXES, scatter_dimension=0, tiled=True
        ).astype(F32)

    def sum_parts(values):
        if paired:
            theirs = other_core(jnp.stack(values))
            return [values[0] + theirs[1], values[1] + theirs[0]]
        return [lax.psum(values[0], PART_AXES)]

    def product(left, right):
        return sum(dot(a, b, ((0,), (0,))) for a, b in zip(left, right)).astype(BF16)

    def scatter(total):
        return lax.psum_scatter(total, WEIGHT_AXES, scatter_dimension=0, tiled=True)

    def scatter_fast(total, splits):
        bits = list(range(ranks.bit_length() - 1))
        orders = [bits, [bits[1], bits[0]] + bits[2:]]
        width = total.shape[1] // splits
        pieces = [
            halving_sum(total[:, n * width : (n + 1) * width], ranks, orders[n % 2])
            for n in range(splits)
        ]
        return pieces[0] if splits == 1 else jnp.concatenate(pieces, axis=1)

    core = lax.axis_index("c")
    ranks = lax.axis_size("p") * lax.axis_size("h")
    depth, _, feat_width = w_qkv.shape
    model = depth * ranks
    parts = 2 if paired else 1

    small = jnp.concatenate([gain_attn, gain_post, gain_ffn, gain_mid])
    columns = -(-small.shape[0] // depth)
    small = jnp.pad(small, (0, columns * depth - small.shape[0])).reshape(depth, columns)
    small = jnp.pad(small, ((0, 0), (0, LANES - columns)))
    first = jnp.concatenate([w_qkv.reshape(depth, 3 * feat_width), small], axis=1)
    first, tokens, scale, w_out_own, w_in_own, w_back_own = (
        exchange(first),
        exchange(tokens),
        exchange(head_scale),
        exchange(w_out),
        exchange(w_in),
        exchange(w_back),
    )

    def gather(a):
        return lax.all_gather(a, WEIGHT_AXES, axis=0, tiled=True)

    first = gather(first)
    w_mix, w_up, w_down = gather(w_out_own), gather(w_in_own), gather(w_back_own)
    w_proj = first[:, : 3 * feat_width]
    small = first[:, 3 * feat_width : 3 * feat_width + columns].astype(F32)
    small = small.reshape(ranks, depth * columns)
    mid_rows = gain_mid.shape[0]
    g_attn, g_post, g_ffn = (
        small[:, n * depth : (n + 1) * depth].reshape(1, model) for n in range(3)
    )
    g_mid = small[:, 3 * depth : 3 * depth + mid_rows].reshape(1, ranks * mid_rows)
    hidden = ranks * mid_rows * lax.axis_size(PART_AXES)

    inputs = tokens.astype(F32)
    rows = inputs.shape[0]
    if paired:
        offs = jnp.stack([core * rows, (1 - core) * rows]).astype(jnp.int32)
    else:
        offs = jnp.zeros((1,), jnp.int32)
    column_scale = jnp.repeat(scale.astype(F32), HD)[None, :]

    norm_attn, inv_attn = normalize(inputs)
    gathered = spread_tokens((norm_attn * g_attn).astype(BF16))
    projected = [dot(part, w_proj).astype(BF16) for part in gathered]
    attended, scaled, lse = attn_forward(offs, projected, column_scale)
    mixed_sum = collect_tokens(lambda t, kind: dot(scaled[t], w_mix).astype(kind))
    norm_post, inv_post = normalize(mixed_sum)
    middle = inputs + norm_post * g_post
    norm_ffn, inv_ffn = normalize(middle)
    gathered_ffn = spread_tokens((norm_ffn * g_ffn).astype(BF16))
    units = w_up.shape[1]
    part_rows = gathered_ffn[0].shape[0]
    wide = ((part_rows, units), BF16, "rows")
    narrow = ((8, part_rows), F32, "columns")
    raised = [
        row_call(
            up_kernel, "ffn_up", [(part, "rows"), (w_up, "whole")], [wide, wide, narrow]
        )
        for part in gathered_ffn
    ]
    active, slope = [r[0] for r in raised], [r[1] for r in raised]
    sums_mid = sum_parts([r[2] for r in raised])
    fed_down = [None] * parts

    def lower(t, kind):
        fed_down[t], out = row_call(
            functools.partial(down_kernel, hidden),
            "ffn_down",
            [(active[t], "rows"), (sums_mid[t], "columns"), (g_mid, "whole"), (w_down, "whole")],
            [wide, ((part_rows, model), kind, "rows")],
        )
        return out

    output = middle + collect_tokens(lower)
    output = exchange(output.astype(BF16))

    cotangent = exchange(cotangent)
    grad_top = cotangent.astype(F32)
    grad_full = spread_tokens(cotangent)
    grad_down = product(fed_down, grad_full)
    grad_down, grad_full = lax.optimization_barrier((grad_down, grad_full))
    grad_down = scatter(grad_down)
    lowered_back = [
        row_call(
            functools.partial(down_back_kernel, hidden),
            "ffn_down_back",
            [
                (grad_full[t], "rows"),
                (w_down, "whole"),
                (active[t], "rows"),
                (sums_mid[t], "columns"),
                (g_mid, "whole"),
            ],
            [wide, narrow, ((8, units), F32, "whole")],
        )
        for t in range(parts)
    ]
    grad_gmid = sum(jnp.sum(r[2], axis=0) for r in lowered_back)
    moments = sum_parts([r[1] for r in lowered_back])
    grad_upper = [None] * parts

    def raise_back(t, kind):
        grad_upper[t], out = row_call(
            functools.partial(up_back_kernel, hidden),
            "ffn_up_back",
            [
                (lowered_back[t][0], "rows"),
                (active[t], "rows"),
                (slope[t], "rows"),
                (sums_mid[t], "columns"),
                (moments[t], "columns"),
                (w_up, "whole"),
            ],
            [wide, ((part_rows, model), kind, "rows")],
        )
        return out

    grad_entry_ffn = collect_tokens(raise_back)
    grad_up = scatter(product(gathered_ffn, grad_upper))
    grad_gffn = jnp.sum(grad_entry_ffn * norm_ffn, axis=0)
    grad_middle = grad_top + norm_back(grad_entry_ffn * g_ffn, norm_ffn, inv_ffn)
    grad_gpost = jnp.sum(grad_middle * norm_post, axis=0)
    grad_mixed = norm_back(grad_middle * g_post, norm_post, inv_post).astype(BF16)
    grad_mfull = spread_tokens(grad_mixed)
    grad_mix = scatter_fast(product(scaled, grad_mfull), 1)
    grad_scaled = [dot(g, w_mix, ((1,), (1,))) for g in grad_mfull]
    grad_heads = sum(
        jnp.sum(jnp.sum(g * a.astype(F32), axis=0).reshape(-1, HD), axis=1)
        for g, a in zip(grad_scaled, attended)
    )
    grad_attended = [(g * column_scale).astype(BF16) for g in grad_scaled]
    grad_proj = attn_backward(offs, projected, grad_attended, attended, lse)
    grad_wproj = scatter_fast(product(gathered, grad_proj), 2)
    grad_entry_attn = collect_tokens(
        lambda t, kind: dot(grad_proj[t], w_proj, ((1,), (1,))).astype(kind)
    )
    grad_gattn = jnp.sum(grad_entry_attn * norm_attn, axis=0)
    grad_inputs = grad_middle + norm_back(grad_entry_attn * g_attn, norm_attn, inv_attn)
    grad_inputs = exchange(grad_inputs.astype(BF16))

    gains = jnp.concatenate([grad_gattn, grad_gpost, grad_gffn])
    own = doubling_sum(jnp.concatenate([gains, grad_gmid, grad_heads]), ranks)
    device_dp = lax.axis_index(("p", "c"))
    device_mp = lax.axis_index(("h", "l"))
    if paired:
        theirs = other_core(own)
        gains = own[: 3 * model] + theirs[: 3 * model]
        own = jnp.where(core == lax.axis_index("h"), own, theirs)[3 * model :]
    else:
        gains = lax.psum(own[: 3 * model], PART_AXES)
        own = exchange(own[3 * model :])
    short = depth // lax.axis_size(PART_AXES)
    starts = device_dp * depth + device_mp * short
    gains = [
        lax.dynamic_slice_in_dim(gains, n * model + starts, short) for n in range(3)
    ]
    grad_mid = lax.dynamic_slice_in_dim(own, device_dp * mid_rows, mid_rows)
    grad_scale = own[grad_gmid.shape[0] :]
    return (
        output,
        grad_inputs,
        exchange(grad_wproj.astype(BF16)).astype(F32).reshape(depth, 3, feat_width),
        exchange(grad_mix.astype(BF16)).astype(F32),
        exchange(grad_up).astype(F32),
        exchange(grad_down).astype(F32),
        *gains,
        grad_mid,
        grad_scale,
    )


def solution(mesh):
    data, split = mesh.shape["dp"], mesh.shape["mp"]
    named = Mesh(mesh.devices.reshape(data // 2, 2, 2, split // 2), ALL_AXES)
    dp, mp = ("p", "c"), ("h", "l")
    specs = (
        P(dp + mp, None),
        P(dp, None, mp),
        P(mp + dp, None),
        P(dp, mp),
        P(mp + dp, None),
    )
    return jax.shard_map(
        functools.partial(body, split == 2),
        mesh=named,
        in_specs=specs + (P(dp), P(dp), P(dp), P(mp + dp), P(mp), P(dp + mp, None)),
        out_specs=specs[:1]
        + specs
        + (P(dp + mp), P(dp + mp), P(dp + mp), P(mp + dp), P(mp)),
        check_vma=False,
    )
```
